32 devices in a mesh: dp: 8 (over z, x), lat: 4 (over y, core).
Axes of the slice: x: 2, y: 2, z: 4, core: 2. Of those that a mesh axis runs over, the one named last changes fastest.
Arguments:
- tokens: bfloat16 [24576, 512], P(('dp', 'lat')), may hold values from -6 to 6
- latents: bfloat16 [1536, 1024], P(('dp', 'lat')), may hold values from -6 to 6
- gain_self: float32 [512], replicated, may hold values from 0.1 to 1.9
- w_qkv_tok: bfloat16 [512, 1536], replicated, may hold values from -1 to 1
- w_o_tok: bfloat16 [512, 512], replicated, may hold values from -0.25 to 0.25
- gain_read: float32 [512], replicated, may hold values from 0.1 to 1.9
- w_kv_read: bfloat16 [512, 2048], replicated, may hold values from -1 to 1
- gain_lat: float32 [1024], replicated, may hold values from 0.1 to 1.9
- w_q_read: bfloat16 [1024, 1024], replicated, may hold values from -1 to 1
- gain_glob: float32 [1024], replicated, may hold values from 0.1 to 1.9
- w_qkv_glob: bfloat16 [3, 1024, 1024], P(None, None, 'lat'), may hold values from -1 to 1
- w_o_glob: bfloat16 [1024, 1024], P('lat'), may hold values from -0.375 to 0.375
- gain_write: float32 [512], replicated, may hold values from 0.1 to 1.9
- w_q_write: bfloat16 [512, 512], replicated, may hold values from -1 to 1
- gain_wlat: float32 [1024], replicated, may hold values from 0.1 to 1.9
- w_kv_write: bfloat16 [1024, 1024], replicated, may hold values from -1 to 1
Outputs:
- tokens_out: bfloat16 [24576, 512], P(('dp', 'lat'))
- latents_out: bfloat16 [1536, 1024], P(('dp', 'lat'))
The draws below stay inside these ranges and needn't reach their ends.
All inputs are finite; a program needn't handle non-finite values.
Results may differ from the reference program's by a relative error of at most 0.015.
Values may be sent and summed in bfloat16 or wider, within the bound.
A program may use at most 128 MiB of HBM per device.

```python
import jax
import jax.numpy as jnp
from jax import lax

D = 512
DL = 1024
HEAD = 64
G = 256
NLAT = 16
TOKENS = 24576
LATENTS = 1536


image_count = 64


def spread_weight(key, salt, shape, fan_in):
    return jax.random.truncated_normal(jax.random.fold_in(key, salt), -6.0, 6.0, shape, jnp.float32) * fan_in ** (-0.5)


def activations(key, salt, rows, width):
    noise = jax.random.truncated_normal(jax.random.fold_in(key, salt), -6.0, 6.0, (rows, width), jnp.float32)
    return noise


def image_part(key, salt, rows, width):
    index = jnp.arange(rows, dtype=jnp.int32) * image_count // rows
    directions = jax.random.truncated_normal(jax.random.fold_in(key, salt), -4.0, 4.0, (image_count, width), jnp.float32)
    amplitude = jax.random.uniform(jax.random.fold_in(key, salt + 1), (image_count,), jnp.float32, 0.5, 1.0)
    return directions[index] * amplitude[index][:, None]


def draw_tokens(key, part):
    values = activations(key, 21, TOKENS, D)
    return values.astype(jnp.bfloat16)


def draw_latents(key, part):
    values = activations(key, 22, LATENTS, DL)
    values = values + image_part(key, 23, LATENTS, DL)
    values = jnp.clip(values, -6.0, 6.0)
    return values.astype(jnp.bfloat16)


def draw_w_qkv_tok(key, part):
    full = spread_weight(key, 31, (D, 3 * D), D)
    return full.astype(jnp.bfloat16)


def draw_w_q_read(key, part):
    full = spread_weight(key, 32, (DL, DL), DL)
    return full.astype(jnp.bfloat16)


def draw_w_kv_read(key, part):
    full = spread_weight(key, 33, (D, 2 * DL), D)
    return full.astype(jnp.bfloat16)


def draw_w_qkv_glob(key, part):
    factors = jnp.array([1.5, 1.5, 1.0], jnp.float32)
    full = spread_weight(key, 35, (3, DL, DL), DL) * factors[:, None, None]
    return full.astype(jnp.bfloat16)


def draw_w_q_write(key, part):
    full = spread_weight(key, 36, (D, D), D)
    return full.astype(jnp.bfloat16)


def draw_w_kv_write(key, part):
    full = spread_weight(key, 37, (DL, 2 * D), DL)
    return full.astype(jnp.bfloat16)


def steps_of(stream_key, shape, cuts, least, largest):
    factor_of = 1.0
    for position, parts in cuts:
        steps = jax.random.uniform(jax.random.fold_in(jax.random.fold_in(stream_key, 6), position), (parts,), jnp.float32, least / len(cuts), largest / len(cuts))
        factor_of = factor_of * jnp.repeat(jnp.exp(steps), shape[position] // parts).reshape((-1,) + (1,) * (len(shape) - 1 - position))
    return factor_of


def centred(key, extent, spread, reach, pieces=(), kind=jnp.bfloat16):
    entries = spread * jax.random.normal(key, extent, jnp.float32)
    if pieces:
        entries = entries * steps_of(key, extent, pieces, -0.22, 0.18)
    return jnp.clip(entries, -reach, reach).astype(kind)


def setup_inputs(seed: int = 0) -> dict:
    seeds = jax.random.split(jax.random.key(seed), 17)
    tokens = draw_tokens(jax.random.fold_in(seeds[16], 71), 0)
    latents = draw_latents(jax.random.fold_in(seeds[16], 71), 0)
    gain_self = jnp.clip(1.0 + 0.18 * jax.random.normal(seeds[2], (D,), jnp.float32), 0.1, 1.9)
    w_qkv_tok = draw_w_qkv_tok(jax.random.fold_in(seeds[16], 71), 0)
    w_o_tok = centred(seeds[4], (D, D), D ** -0.5, 0.25)
    gain_read = jnp.clip(1.0 + 0.18 * jax.random.normal(seeds[5], (D,), jnp.float32), 0.1, 1.9)
    w_kv_read = draw_w_kv_read(jax.random.fold_in(seeds[16], 71), 0)
    gain_lat = jnp.clip(1.0 + 0.18 * jax.random.normal(seeds[7], (DL,), jnp.float32), 0.1, 1.9)
    w_q_read = draw_w_q_read(jax.random.fold_in(seeds[16], 71), 0)
    gain_glob = jnp.clip(1.0 + 0.18 * jax.random.normal(seeds[9], (DL,), jnp.float32), 0.1, 1.9)
    w_qkv_glob = draw_w_qkv_glob(jax.random.fold_in(seeds[16], 71), 0)
    w_o_glob = centred(seeds[11], (DL, DL), (DL // 4) ** -0.5, 0.375, ((0, 4),))
    gain_write = jnp.clip(1.0 + 0.18 * jax.random.normal(seeds[12], (D,), jnp.float32), 0.1, 1.9)
    w_q_write = draw_w_q_write(jax.random.fold_in(seeds[16], 71), 0)
    gain_wlat = jnp.clip(1.0 + 0.18 * jax.random.normal(seeds[14], (DL,), jnp.float32), 0.1, 1.9)
    w_kv_write = draw_w_kv_write(jax.random.fold_in(seeds[16], 71), 0)
    return dict(tokens=tokens, latents=latents, gain_self=gain_self, w_qkv_tok=w_qkv_tok, w_o_tok=w_o_tok, gain_read=gain_read, w_kv_read=w_kv_read, gain_lat=gain_lat, w_q_read=w_q_read, gain_glob=gain_glob, w_qkv_glob=w_qkv_glob, w_o_glob=w_o_glob, gain_write=gain_write, w_q_write=w_q_write, gain_wlat=gain_wlat, w_kv_write=w_kv_write)


def rms_norm(values, gain):
    floats = values.astype(jnp.float32)
    factor = lax.rsqrt(lax.optimization_barrier(jnp.mean(floats * floats, axis=-1, keepdims=True)) + 1e-06)
    return (floats * factor * gain).astype(jnp.bfloat16)

def attend(query, keys, values):
    scores = jnp.einsum('qhe,khe->hqk', query.astype(jnp.float32), keys.astype(jnp.float32)) * HEAD ** (-0.5)
    peak = lax.optimization_barrier(jnp.max(scores, axis=-1, keepdims=True))
    weights = jnp.exp(scores - peak)
    total = lax.optimization_barrier(jnp.sum(weights, axis=-1))
    rounded = lax.optimization_barrier(weights.astype(jnp.bfloat16)).astype(jnp.float32)
    mixed = jnp.einsum('hqk,khe->hqe', rounded, values.astype(jnp.float32))
    return jnp.transpose(mixed / total[:, :, None], (1, 0, 2))

def front(inputs, gain_self, w_qkv_tok, w_o_tok, gain_read, w_kv_read, gain_lat, w_q_read):
    group, lat_rows = inputs
    rows = group.shape[0]
    packed = jnp.dot(rms_norm(group, gain_self), w_qkv_tok, preferred_element_type=jnp.float32)
    packed = packed.astype(jnp.bfloat16).reshape(rows, 3, -1, HEAD)
    mixed = attend(packed[:, 0], packed[:, 1], packed[:, 2]).reshape(rows, -1).astype(jnp.bfloat16)
    tokens_mid = (group.astype(jnp.float32) + jnp.dot(mixed, w_o_tok, preferred_element_type=jnp.float32)).astype(jnp.bfloat16)
    key_vals = jnp.dot(rms_norm(tokens_mid, gain_read), w_kv_read, preferred_element_type=jnp.float32)
    key_vals = key_vals.astype(jnp.bfloat16).reshape(rows, 2, -1, HEAD)
    query = jnp.dot(rms_norm(lat_rows, gain_lat), w_q_read, preferred_element_type=jnp.float32)
    query = query.astype(jnp.bfloat16).reshape(lat_rows.shape[0], -1, HEAD)
    read = attend(query, key_vals[:, 0], key_vals[:, 1]).reshape(lat_rows.shape[0], -1)
    return (tokens_mid, (lat_rows.astype(jnp.float32) + read).astype(jnp.bfloat16))

def back(inputs, gain_write, w_q_write, gain_wlat, w_kv_write):
    tokens_mid, lat_rows = inputs
    rows = tokens_mid.shape[0]
    query = jnp.dot(rms_norm(tokens_mid, gain_write), w_q_write, preferred_element_type=jnp.float32)
    query = query.astype(jnp.bfloat16).reshape(rows, -1, HEAD)
    key_vals = jnp.dot(rms_norm(lat_rows, gain_wlat), w_kv_write, preferred_element_type=jnp.float32)
    key_vals = key_vals.astype(jnp.bfloat16).reshape(lat_rows.shape[0], 2, -1, HEAD)
    written = attend(query, key_vals[:, 0], key_vals[:, 1]).reshape(rows, -1)
    return (tokens_mid.astype(jnp.float32) + written).astype(jnp.bfloat16)

def one_head(inputs):
    query, keys, values = inputs
    scores = jnp.dot(query, keys.T, preferred_element_type=jnp.float32) * HEAD ** (-0.5)
    peak = lax.optimization_barrier(jnp.max(scores, axis=-1, keepdims=True))
    weights = jnp.exp(scores - peak)
    total = lax.optimization_barrier(jnp.sum(weights, axis=-1, keepdims=True))
    mixed = jnp.dot(weights.astype(jnp.bfloat16), values, preferred_element_type=jnp.float32)
    return (mixed / total).astype(jnp.bfloat16)

def reference(tokens, latents, gain_self, w_qkv_tok, w_o_tok, gain_read, w_kv_read, gain_lat, w_q_read, gain_glob, w_qkv_glob, w_o_glob, gain_write, w_q_write, gain_wlat, w_kv_write):
    groups = tokens.reshape(-1, G, D)
    lat_groups = latents.reshape(-1, NLAT, DL)
    tokens_mid, latents_mid = lax.map(lambda pair: front(pair, gain_self, w_qkv_tok, w_o_tok, gain_read, w_kv_read, gain_lat, w_q_read), (groups, lat_groups))
    latents_mid = latents_mid.reshape(-1, DL)
    count = latents_mid.shape[0]
    normed = rms_norm(latents_mid, gain_glob)
    heads = []
    for which in range(3):
        projected = jnp.dot(normed, w_qkv_glob[which], preferred_element_type=jnp.float32).astype(jnp.bfloat16)
        heads.append(jnp.transpose(projected.reshape(count, -1, HEAD), (1, 0, 2)))
    mixed = lax.map(one_head, (heads[0], heads[1], heads[2]))
    mixed = jnp.transpose(mixed, (1, 0, 2)).reshape(count, -1)
    latents_out = (latents_mid.astype(jnp.float32) + jnp.dot(mixed, w_o_glob, preferred_element_type=jnp.float32)).astype(jnp.bfloat16)
    tokens_out = lax.map(lambda pair: back(pair, gain_write, w_q_write, gain_wlat, w_kv_write), (tokens_mid, latents_out.reshape(-1, NLAT, DL)))
    return (tokens_out.reshape(-1, D), latents_out)
```

```python
import functools

import jax
import jax.numpy as jnp
from jax import lax
from jax.experimental import pallas as pl
from jax.experimental.pallas import tpu as pltpu
from jax.sharding import PartitionSpec as P

HEAD = 64
G = 256
NLAT = 16
SCALE = HEAD ** (-0.5)
MESH = pl.DeviceIdType.MESH
F32 = jnp.float32
BF16 = jnp.bfloat16


def rms_norm(values, gain):
    floats = values.astype(F32)
    factor = lax.rsqrt(jnp.mean(floats * floats, axis=-1, keepdims=True) + 1e-06)
    return (floats * factor * gain).astype(BF16)


def dot(a, b):
    return jnp.dot(a, b, preferred_element_type=F32)


def dot_nt(a, b):
    return lax.dot_general(a, b, (((1,), (1,)), ((), ())), preferred_element_type=F32)


def dot_tn(a, b):
    return lax.dot_general(a, b, (((0,), (0,)), ((), ())), preferred_element_type=F32)


def spread_heads(query, count):
    lane_head = lax.broadcasted_iota(jnp.int32, query.shape, 1) // HEAD
    zero = jnp.zeros_like(query)
    return jnp.concatenate([jnp.where(lane_head == h, query, zero) for h in range(count)], axis=0)


def fold_heads(stacked, count):
    rows = stacked.shape[0] // count
    lane_head = lax.broadcasted_iota(jnp.int32, (rows, stacked.shape[1]), 1) // HEAD
    out = stacked[:rows]
    for h in range(1, count):
        out = jnp.where(lane_head == h, stacked[h * rows : (h + 1) * rows], out)
    return out


def softmax_mix(stacked, keys, values):
    scores = dot_nt(stacked, keys)
    peak = jnp.max(scores, axis=-1, keepdims=True)
    weights = jnp.exp(scores - peak)
    total = jnp.sum(weights, axis=-1, keepdims=True)
    return dot(weights.astype(BF16), values) * (1.0 / total)


def kernel(
    dp_count,
    lat_count,
    tok,
    lat_in,
    g_self,
    w_qkv_h,
    w_o_h,
    g_read,
    w_kvr_h,
    g_lat,
    w_qr_h,
    g_glob,
    w_glob_h,
    w_og_h,
    g_write,
    w_qw_h,
    g_wlat,
    w_kvw_h,
    tok_out,
    lat_out,
    w_qkv,
    w_o,
    w_kvr,
    w_qr,
    w_glob,
    w_og,
    w_qw,
    w_kvw,
    mid,
    lmid,
    rq,
    packed,
    mixed,
    kvr,
    gath,
    kv,
    qq,
    msend,
    mrecv,
    lfin,
    load_sem,
    z_send,
    z_recv,
    p_send,
    p_recv,
    c_send,
    c_recv,
    wo_send,
    wo_recv,
    m_send,
    m_recv,
):
    width = tok.shape[1]
    lat_width = lat_in.shape[1]
    groups = tok.shape[0] // G
    lat_rows = lat_in.shape[0]
    nz = dp_count // 2
    dp = lax.axis_index("dp")
    lat = lax.axis_index("lat")
    z, x = dp // 2, dp % 2
    y, core = lat // 2, lat % 2
    dp_x = dp + 1 - 2 * x
    lat_y = (lat + 2) % 4
    partner = lat + 1 - 2 * core
    diag = (partner + 2) % 4
    a = (1 - core) * y + core * x
    b = (1 - core) * x + core * y
    first = ((1 - core) * dp + core * dp_x, (1 - core) * lat_y + core * lat)
    second = ((1 - core) * dp_x + core * dp, (1 - core) * lat + core * lat_y)
    base = (b * 2 + a) * nz
    other = (b * 2 + 1 - a) * nz
    me = base + z

    loads = []
    for i, (src, dst) in enumerate(
        ((w_qkv_h, w_qkv), (w_o_h, w_o), (w_qr_h, w_qr), (w_kvr_h, w_kvr), (w_glob_h, w_glob),
         (w_qw_h, w_qw), (w_kvw_h, w_kvw), (w_og_h, w_og.at[lat]))
    ):
        loads.append(pltpu.make_async_copy(src, dst, load_sem.at[i]))
        loads[-1].start()

    barrier = pltpu.get_barrier_semaphore()

    def greet(offset, carry):
        pl.semaphore_signal(
            barrier, inc=1, device_id=((z + offset) % nz * 2 + x, lat), device_id_type=MESH
        )
        return carry

    lax.fori_loop(1, nz, greet, 0)
    for peer in ((dp_x, lat), (dp, lat_y), (dp, partner), (dp, diag)):
        pl.semaphore_signal(barrier, inc=1, device_id=peer, device_id_type=MESH)
    pl.semaphore_wait(barrier, nz + 3)

    def remote(src, dst, send_sem, recv_sem, peer):
        return pltpu.make_async_remote_copy(
            src_ref=src, dst_ref=dst, send_sem=send_sem, recv_sem=recv_sem, device_id=peer,
            device_id_type=MESH,
        )

    wo_first = [
        remote(w_og_h, w_og.at[lat], wo_send.at[0], wo_recv.at[0], (dp, partner)),
        remote(w_og_h, w_og.at[lat], wo_send.at[1], wo_recv.at[1], (dp, lat_y)),
    ]
    wo_relay = remote(w_og.at[lat_y], w_og.at[lat_y], wo_send.at[2], wo_recv.at[2], (dp, partner))
    for copy in wo_first:
        copy.start()

    def piece(g, start, count):
        return gath.at[g, core, pl.ds(start, count)]

    def along(ref, send_sem, recv_sem, peer):
        return remote(ref, ref, send_sem, recv_sem, peer)

    to_first = [along(piece(g, base, nz), p_send.at[g, 0], p_recv.at[g, 0], first) for g in range(groups)]
    to_second = [
        along(piece(g, b * 2 * nz, 2 * nz), p_send.at[g, 1], p_recv.at[g, 1], second)
        for g in range(groups)
    ]
    shares = [
        [
            along(piece(g, start, count), c_send.at[g, i], c_recv.at[g, i], (dp, partner))
            for i, (start, count) in enumerate(
                ((base, nz), (other, nz), ((1 - b) * 2 * nz, 2 * nz))
            )
        ]
        for g in range(groups)
    ]

    def z_start(g):
        def one(offset, carry):
            remote(
                gath.at[g, core, me], gath.at[g, core, me], z_send.at[g], z_recv.at[g],
                ((z + offset) % nz * 2 + x, lat),
            ).start()
            return carry

        lax.fori_loop(1, nz, one, 0)

    def z_wait(g, sem):
        ref = piece(g, base, nz - 1)
        pltpu.make_async_copy(ref, ref, sem.at[g]).wait()

    def stage_one(g):
        z_wait(g, z_recv)
        to_first[g].start()
        shares[g][0].start()

    def stage_two(g):
        to_first[g].wait_recv()
        to_second[g].start()
        shares[g][1].start()

    def stage_three(g):
        to_second[g].wait_recv()
        shares[g][2].start()

    def self_part(g):
        rows = pl.ds(g * G, G)
        group = tok[rows, :]
        normed = rms_norm(group, g_self[...])
        if g == 0:
            loads[0].wait()
        packed[...] = dot(normed, w_qkv[...]).astype(BF16)
        for pair in range(width // (2 * HEAD)):
            at = pair * 2 * HEAD
            query = packed[:, at : at + 2 * HEAD] * jnp.asarray(SCALE, BF16)
            keys = packed[:, width + at : width + at + 2 * HEAD]
            values = packed[:, 2 * width + at : 2 * width + at + 2 * HEAD]
            out = softmax_mix(spread_heads(query, 2), keys, values)
            mixed[:, at : at + 2 * HEAD] = fold_heads(out, 2).astype(BF16)
        if g == 0:
            loads[1].wait()
        mid[rows, :] = (group.astype(F32) + dot(mixed[...], w_o[...])).astype(BF16)

    def read_part(g):
        if g == 0:
            loads[2].wait()
            query = dot(rms_norm(lat_in[...], g_lat[...]), w_qr[...]).astype(BF16)
            rq[...] = query * jnp.asarray(SCALE, BF16)
            loads[3].wait()
        rows = pl.ds(g * G, G)
        lrows = pl.ds(g * NLAT, NLAT)
        kvr[...] = dot(rms_norm(mid[rows, :], g_read[...]), w_kvr[...]).astype(BF16)
        quad = 4 * HEAD
        for at in range(0, lat_width, quad):
            out = softmax_mix(
                spread_heads(rq[lrows, at : at + quad], 4),
                kvr[:, at : at + quad],
                kvr[:, lat_width + at : lat_width + at + quad],
            )
            lmid[lrows, at : at + quad] = (
                lat_in[lrows, at : at + quad].astype(F32) + fold_heads(out, 4)
            ).astype(BF16)
        gath[g, core, me] = rms_norm(lmid[lrows, :], g_glob[...])
        z_start(g)

    pending = []

    def advance():
        for i, (g, stage) in enumerate(pending):
            if stage < 3:
                (stage_one, stage_two, stage_three)[stage](g)
                pending[i] = (g, stage + 1)

    for g in range(groups):
        self_part(g)
        advance()
        read_part(g)
        advance()
        if g == groups - 2:
            wo_first[1].wait_recv()
            wo_relay.start()
        pending.append((g, 0))

    block_rows = 4 * nz * NLAT
    tile = min(block_rows, G)
    blocks = tile // NLAT

    def project(g, c):
        def one(i, carry):
            rows = gath[g, c, pl.ds(i * blocks, blocks)].reshape(tile, lat_width)
            at = pl.multiple_of((g * 2 + c) * block_rows + i * tile, tile)
            kv[0, pl.ds(at, tile), :] = dot(rows, w_glob[1]).astype(BF16)
            kv[1, pl.ds(at, tile), :] = dot(rows, w_glob[2]).astype(BF16)
            return carry

        lax.fori_loop(0, block_rows // tile, one, 0)

    loads[5].wait()
    for g in range(groups):
        rows = pl.ds(g * G, G)
        query = dot(rms_norm(mid[rows, :], g_write[...]), w_qw[...]).astype(BF16)
        tok_out[rows, :] = query * jnp.asarray(SCALE, BF16)
    advance()
    loads[4].wait()
    for g in range(groups):
        while pending[g][1] < 3:
            advance()
        for c in range(3):
            shares[g][c].wait_recv()
        project(g, 0)
        project(g, 1)

    own = []
    for l in range(lat_count):
        ly, lc = l // 2, l % 2
        index = ((x * 2 + ly) if lc == 0 else (ly * 2 + x)) * nz + z
        for g in range(groups):
            own.append(gath[g, lc, index])
    query = dot(jnp.concatenate(own, axis=0), w_glob[0]).astype(BF16) * jnp.asarray(SCALE, BF16)
    heads = query.shape[1] // HEAD
    qq[...] = spread_heads(query, heads)
    part = lat_rows * lat_count if kv.shape[1] * lat_rows * lat_count <= 2**20 else lat_rows

    def attend(i, carry):
        rows = pl.ds(pl.multiple_of(i * part, part), part)
        qq[rows, :] = softmax_mix(qq[rows, :], kv[0], kv[1]).astype(BF16)
        return carry

    lax.fori_loop(0, qq.shape[0] // part, attend, 0)
    result = fold_heads(qq[...], heads)
    for l in range(lat_count):
        msend[l] = result[l * lat_rows : (l + 1) * lat_rows]
    mix_copies = []
    for i, peer in enumerate((partner, lat_y, diag)):
        mix_copies.append(remote(msend.at[peer], mrecv.at[lat], m_send.at[i], m_recv.at[i], (dp, peer)))
        mix_copies[-1].start()
    mrecv[lat] = msend[lat]
    loads[7].wait()
    loads[6].wait()
    wo_first[0].wait_recv()
    wo_relay.wait_recv()
    for copy in mix_copies:
        copy.wait_recv()
    total = dot(mrecv[0], w_og[0])
    for l in range(1, lat_count):
        total = total + dot(mrecv[l], w_og[l])
    final = (lmid[...].astype(F32) + total).astype(BF16)
    lat_out[...] = final
    lfin[...] = dot(rms_norm(final, g_wlat[...]), w_kvw[...]).astype(BF16)

    heads = width // HEAD
    for g in range(groups):
        rows = pl.ds(g * G, G)
        lrows = pl.ds(g * NLAT, NLAT)
        keys = spread_heads(lfin[lrows, :width], heads)
        values = spread_heads(lfin[lrows, width:], heads)
        scores = dot_nt(keys, tok_out[rows, :]).reshape(heads, NLAT, G)
        peak = jnp.max(scores, axis=1, keepdims=True)
        weights = jnp.exp(scores - peak)
        weights = weights * (1.0 / jnp.sum(weights, axis=1, keepdims=True))
        written = dot_tn(weights.reshape(heads * NLAT, G).astype(BF16), values)
        tok_out[rows, :] = (mid[rows, :].astype(F32) + written).astype(BF16)

    for copy in wo_first + [wo_relay] + mix_copies:
        copy.wait_send()
    for g in range(groups):
        z_wait(g, z_send)
        to_first[g].wait_send()
        to_second[g].wait_send()
        for copy in shares[g]:
            copy.wait_send()


def local(
    tokens, latents, gain_self, w_qkv_tok, w_o_tok, gain_read, w_kv_read, gain_lat, w_q_read,
    gain_glob, w_qkv_glob, w_o_glob, gain_write, w_q_write, gain_wlat, w_kv_write,
):
    dp_count = lax.axis_size("dp")
    lat_count = lax.axis_size("lat")
    rows, width = tokens.shape
    lat_rows, lat_width = latents.shape
    groups = rows // G
    here = w_qkv_glob.shape[2]
    nz = dp_count // 2
    all_rows = lat_rows * dp_count * lat_count
    vmem = pl.BlockSpec(memory_space=pltpu.VMEM)
    hbm = pl.BlockSpec(memory_space=pl.ANY)
    dma = pltpu.SemaphoreType.DMA
    return pl.pallas_call(
        functools.partial(kernel, dp_count, lat_count),
        out_shape=(
            jax.ShapeDtypeStruct(tokens.shape, BF16),
            jax.ShapeDtypeStruct(latents.shape, BF16),
        ),
        in_specs=[vmem, vmem, vmem, hbm, hbm, vmem, hbm, vmem, hbm, vmem, hbm, hbm, vmem, hbm, vmem, hbm],
        out_specs=(vmem, vmem),
        scratch_shapes=[
            pltpu.VMEM(w_qkv_tok.shape, BF16),
            pltpu.VMEM(w_o_tok.shape, BF16),
            pltpu.VMEM(w_kv_read.shape, BF16),
            pltpu.VMEM(w_q_read.shape, BF16),
            pltpu.VMEM(w_qkv_glob.shape, BF16),
            pltpu.VMEM((lat_count,) + w_o_glob.shape, BF16),
            pltpu.VMEM(w_q_write.shape, BF16),
            pltpu.VMEM(w_kv_write.shape, BF16),
            pltpu.VMEM(tokens.shape, BF16),
            pltpu.VMEM(latents.shape, BF16),
            pltpu.VMEM(latents.shape, BF16),
            pltpu.VMEM((G, w_qkv_tok.shape[1]), BF16),
            pltpu.VMEM((G, width), BF16),
            pltpu.VMEM((G, w_kv_read.shape[1]), BF16),
            pltpu.VMEM((groups, 2, 4 * nz, NLAT, lat_width), BF16),
            pltpu.VMEM((2, all_rows, here), BF16),
            pltpu.VMEM((lat_rows * lat_count * (here // HEAD), here), BF16),
            pltpu.VMEM((lat_count, lat_rows, here), BF16),
            pltpu.VMEM((lat_count, lat_rows, here), BF16),
            pltpu.VMEM((lat_rows, w_kv_write.shape[1]), BF16),
            dma((8,)),
            dma((groups,)),
            dma((groups,)),
            dma((groups, 2)),
            dma((groups, 2)),
            dma((groups, 3)),
            dma((groups, 3)),
            dma((3,)),
            dma((3,)),
            dma((3,)),
            dma((3,)),
        ],
        compiler_params=pltpu.CompilerParams(
            collective_id=0, has_side_effects=True, vmem_limit_bytes=67043328
        ),
    )(
        tokens, latents, gain_self[None], w_qkv_tok, w_o_tok, gain_read[None], w_kv_read,
        gain_lat[None], w_q_read, gain_glob[None], w_qkv_glob, w_o_glob, gain_write[None],
        w_q_write, gain_wlat[None], w_kv_write,
    )


def solution(mesh):
    rows = P(("dp", "lat"), None)
    whole = P()
    placed = (
        rows, rows, whole, whole, whole, whole, whole, whole, whole, whole,
        P(None, None, "lat"), P("lat", None), whole, whole, whole, whole,
    )
    return jax.shard_map(
        local, mesh=mesh, in_specs=placed, out_specs=(rows, rows), check_vma=False
    )
```

```python
import functools

import jax
import jax.numpy as jnp
from jax import lax
from jax.experimental import pallas as pl
from jax.experimental.pallas import tpu as pltpu
from jax.sharding import PartitionSpec as P

HEAD = 64
G = 256
NLAT = 16
SCALE = HEAD ** (-0.5)
MESH = pl.DeviceIdType.MESH
PARTS = 4
F32 = jnp.float32
BF16 = jnp.bfloat16


def rms_norm(values, gain):
    floats = values.astype(F32)
    factor = lax.rsqrt(jnp.mean(floats * floats, axis=-1, keepdims=True) + 1e-06)
    return (floats * factor * gain).astype(BF16)


def dot(a, b):
    return jnp.dot(a, b, preferred_element_type=F32)


def dot_nt(a, b):
    return lax.dot_general(a, b, (((1,), (1,)), ((), ())), preferred_element_type=F32)


def dot_tn(a, b):
    return lax.dot_general(a, b, (((0,), (0,)), ((), ())), preferred_element_type=F32)


def spread_heads(query, count):
    lane_head = lax.broadcasted_iota(jnp.int32, query.shape, 1) // HEAD
    zero = jnp.zeros_like(query)
    return jnp.concatenate([jnp.where(lane_head == h, query, zero) for h in range(count)], axis=0)


def fold_heads(stacked, count):
    rows = stacked.shape[0] // count
    lane_head = lax.broadcasted_iota(jnp.int32, (rows, stacked.shape[1]), 1) // HEAD
    out = stacked[:rows]
    for h in range(1, count):
        out = jnp.where(lane_head == h, stacked[h * rows : (h + 1) * rows], out)
    return out


def softmax_mix(stacked, keys, values):
    scores = dot_nt(stacked, keys)
    peak = jnp.max(scores, axis=-1, keepdims=True)
    weights = jnp.exp(scores - peak)
    total = jnp.sum(weights, axis=-1, keepdims=True)
    return dot(weights.astype(BF16), values) * (1.0 / total)


def kernel(
    dp_count,
    lat_count,
    tok,
    lat_in,
    g_self,
    w_qkv_h,
    w_o_h,
    g_read,
    w_kvr_h,
    g_lat,
    w_qr_h,
    g_glob,
    w_glob_h,
    w_og_h,
    g_write,
    w_qw_h,
    g_wlat,
    w_kvw_h,
    tok_out,
    lat_out,
    w_qkv,
    w_o,
    w_kvr,
    w_qr,
    w_glob,
    w_og,
    w_qw,
    w_kvw,
    mid,
    lmid,
    rq,
    packed,
    mixed,
    kvr,
    gath,
    kv,
    qq,
    msend,
    mrecv,
    lfin,
    top,
    norm,
    acc,
    load_sem,
    z_send,
    z_recv,
    f_send,
    f_recv,
    s_send,
    s_recv,
    c_send,
    c_recv,
    wo_send,
    wo_recv,
    m_send,
    m_recv,
):
    width = tok.shape[1]
    lat_width = lat_in.shape[1]
    groups = tok.shape[0] // G
    lat_rows = lat_in.shape[0]
    nz = dp_count // 2
    dp = lax.axis_index("dp")
    lat = lax.axis_index("lat")
    z, x = dp // 2, dp % 2
    y, core = lat // 2, lat % 2
    dp_x = dp + 1 - 2 * x
    lat_y = (lat + 2) % 4
    partner = lat + 1 - 2 * core
    diag = (partner + 2) % 4
    a = (1 - core) * y + core * x
    b = (1 - core) * x + core * y
    first = ((1 - core) * dp + core * dp_x, (1 - core) * lat_y + core * lat)
    second = ((1 - core) * dp_x + core * dp, (1 - core) * lat + core * lat_y)
    base = (b * 2 + a) * nz
    other = (b * 2 + 1 - a) * nz
    me = base + z
    far = (1 - 2 * b) * 2 * nz
    run = nz // PARTS

    loads = []
    for i, (src, dst) in enumerate(
        ((w_qkv_h, w_qkv), (w_o_h, w_o), (w_qr_h, w_qr), (w_kvr_h, w_kvr), (w_glob_h, w_glob),
         (w_qw_h, w_qw), (w_kvw_h, w_kvw), (w_og_h, w_og.at[lat]))
    ):
        loads.append(pltpu.make_async_copy(src, dst, load_sem.at[i]))
        loads[-1].start()

    barrier = pltpu.get_barrier_semaphore()

    def greet(offset, carry):
        pl.semaphore_signal(
            barrier, inc=1, device_id=((z + offset) % nz * 2 + x, lat), device_id_type=MESH
        )
        return carry

    lax.fori_loop(1, nz, greet, 0)
    for peer in ((dp_x, lat), (dp, lat_y), (dp, partner), (dp, diag)):
        pl.semaphore_signal(barrier, inc=1, device_id=peer, device_id_type=MESH)
    pl.semaphore_wait(barrier, nz + 3)

    def remote(src, dst, send_sem, recv_sem, peer):
        return pltpu.make_async_remote_copy(
            src_ref=src, dst_ref=dst, send_sem=send_sem, recv_sem=recv_sem, device_id=peer,
            device_id_type=MESH,
        )

    wo_first = [
        remote(w_og_h, w_og.at[lat], wo_send.at[0], wo_recv.at[0], (dp, partner)),
        remote(w_og_h, w_og.at[lat], wo_send.at[1], wo_recv.at[1], (dp, lat_y)),
    ]
    wo_relay = remote(w_og.at[lat_y], w_og.at[lat_y], wo_send.at[2], wo_recv.at[2], (dp, partner))
    for copy in wo_first:
        copy.start()

    def piece(g, start, count):
        return gath.at[g, core, pl.ds(start, count)]

    def along(ref, send_sem, recv_sem, peer):
        return remote(ref, ref, send_sem, recv_sem, peer)

    def on_first(g, p):
        return along(
            piece(g, base + p * run, run), f_send.at[g, p], f_recv.at[g, p], first
        )

    def on_second(g, half, p):
        start = base + (other - base) * half + p * run
        k = half * PARTS + p
        return along(piece(g, start, run), s_send.at[g, k], s_recv.at[g, k], second)

    def share(g, line, p):
        start = (base, other, base + far, other + far)[line] + p * run
        k = line * PARTS + p
        return along(
            piece(g, start, run), c_send.at[g, k], c_recv.at[g, k], (dp, partner)
        )

    def z_copy(g, offset):
        return remote(
            gath.at[g, core, me], gath.at[g, core, me], z_send.at[g, (z + offset) % nz],
            z_recv.at[g, z], ((z + offset) % nz * 2 + x, lat),
        )

    def each(low, high, body):
        def one(i, carry):
            body(i)
            return carry

        lax.fori_loop(low, high, one, 0)

    def z_start(g):
        each(1, nz, lambda offset: z_copy(g, offset).start())

    def z_arrived(g, block):
        ref = piece(g, base + block, 1)

        @pl.when(block != z)
        def _():
            pltpu.make_async_copy(ref, ref, z_recv.at[g, block]).wait()

    def stage_one(g, low, high):
        def body(o):
            p = (z // run + o) % PARTS
            each(0, run, lambda i: z_arrived(g, p * run + i))
            on_first(g, p).start()
            on_second(g, 0, p).start()
            share(g, 0, p).start()

        each(low, high, body)

    def stage_two(g):
        def body(o):
            p = (z // run + o) % PARTS
            on_first(g, p).wait_recv()
            on_second(g, 1, p).start()
            share(g, 1, p).start()

        each(0, PARTS, body)

    def second_arrived(g, half, o):
        p = (z // run + o) % PARTS
        on_second(g, half, p).wait_recv()
        share(g, 2 + half, p).start()

    def stage_three(g):
        for half in range(2):
            each(0, PARTS, lambda o: second_arrived(g, half, o))

    def gathered(g):
        for line in range(4):
            each(0, PARTS, lambda p: share(g, line, p).wait_recv())

    def self_part(g):
        rows = pl.ds(g * G, G)
        group = tok[rows, :]
        normed = rms_norm(group, g_self[...])
        if g == 0:
            loads[0].wait()
        packed[...] = dot(normed, w_qkv[...]).astype(BF16)
        for pair in range(width // (2 * HEAD)):
            at = pair * 2 * HEAD
            query = packed[:, at : at + 2 * HEAD] * jnp.asarray(SCALE, BF16)
            keys = packed[:, width + at : width + at + 2 * HEAD]
            values = packed[:, 2 * width + at : 2 * width + at + 2 * HEAD]
            out = softmax_mix(spread_heads(query, 2), keys, values)
            mixed[:, at : at + 2 * HEAD] = fold_heads(out, 2).astype(BF16)
        if g == 0:
            loads[1].wait()
        mid[rows, :] = (group.astype(F32) + dot(mixed[...], w_o[...])).astype(BF16)

    def read_part(g):
        if g == 0:
            loads[2].wait()
            query = dot(rms_norm(lat_in[...], g_lat[...]), w_qr[...]).astype(BF16)
            rq[...] = query * jnp.asarray(SCALE, BF16)
            loads[3].wait()
        rows = pl.ds(g * G, G)
        lrows = pl.ds(g * NLAT, NLAT)
        kvr[...] = dot(rms_norm(mid[rows, :], g_read[...]), w_kvr[...]).astype(BF16)
        quad = 4 * HEAD
        for at in range(0, lat_width, quad):
            out = softmax_mix(
                spread_heads(rq[lrows, at : at + quad], 4),
                kvr[:, at : at + quad],
                kvr[:, lat_width + at : lat_width + at + quad],
            )
            lmid[lrows, at : at + quad] = (
                lat_in[lrows, at : at + quad].astype(F32) + fold_heads(out, 4)
            ).astype(BF16)
        gath[g, core, me] = rms_norm(lmid[lrows, :], g_glob[...])
        z_start(g)
        stage_one(g, 0, 1)

    last = groups - 1
    for g in range(groups):
        self_part(g)
        if g >= 2:
            stage_one(g - 2, 1, PARTS)
            if g == 2:
                wo_first[1].wait_recv()
                wo_relay.start()
        read_part(g)

    block_rows = 4 * nz * NLAT
    tile = min(block_rows, G)
    blocks = tile // NLAT

    def project(g, c):
        def one(i, carry):
            rows = gath[g, c, pl.ds(i * blocks, blocks)].reshape(tile, lat_width)
            at = pl.multiple_of((g * 2 + c) * block_rows + i * tile, tile)
            kv[0, pl.ds(at, tile), :] = dot(rows, w_glob[1]).astype(BF16)
            kv[1, pl.ds(at, tile), :] = dot(rows, w_glob[2]).astype(BF16)
            return carry

        lax.fori_loop(0, block_rows // tile, one, 0)

    for g in range(last - 1):
        stage_two(g)
    loads[5].wait()
    for g in range(groups):
        rows = pl.ds(g * G, G)
        query = dot(rms_norm(mid[rows, :], g_write[...]), w_qw[...]).astype(BF16)
        tok_out[rows, :] = query * jnp.asarray(SCALE, BF16)
    stage_one(last - 1, 1, PARTS)
    loads[4].wait()
    for g in range(last - 1):
        stage_three(g)
    stage_two(last - 1)
    for g in range(last - 1):
        gathered(g)
        project(g, 0)
        project(g, 1)
    stage_one(last, 1, PARTS)
    stage_two(last)
    stage_three(last - 1)
    gathered(last - 1)
    project(last - 1, 0)
    project(last - 1, 1)
    own_p = z // run

    @pl.when(core == 1)
    def _():
        on_second(last, 0, own_p).wait_recv()
        share(last, 2, own_p).start()
        for line in range(2):
            share(last, line, own_p).wait_recv()

    @pl.when(core == 0)
    def _():
        for line in (0, 2):
            share(last, line, own_p).wait_recv()

    own = []
    for l in range(lat_count):
        ly, lc = l // 2, l % 2
        index = ((x * 2 + ly) if lc == 0 else (ly * 2 + x)) * nz + z
        for g in range(groups):
            own.append(gath[g, lc, index])
    query = dot(jnp.concatenate(own, axis=0), w_glob[0]).astype(BF16) * jnp.asarray(SCALE, BF16)
    heads = query.shape[1] // HEAD
    qq[...] = spread_heads(query, heads)
    early = last * 2 * block_rows
    full = lat_rows * lat_count
    part = full if early * full <= 2**20 else lat_rows

    def attend_early(i, carry):
        rows = pl.ds(pl.multiple_of(i * part, part), part)
        scores = dot_nt(qq[rows, :], kv[0, :early, :])
        peak = jnp.max(scores, axis=-1, keepdims=True)
        weights = jnp.exp(scores - peak)
        top[rows, :] = peak
        norm[rows, :] = jnp.sum(weights, axis=-1, keepdims=True)
        acc[rows, :] = dot(weights.astype(BF16), kv[1, :early, :])
        return carry

    def attend_late(i, carry):
        rows = pl.ds(pl.multiple_of(i * part, part), part)
        scores = dot_nt(qq[rows, :], kv[0, early:, :])
        peak = jnp.maximum(top[rows, :], jnp.max(scores, axis=-1, keepdims=True))
        weights = jnp.exp(scores - peak)
        keep = jnp.exp(top[rows, :] - peak)
        total = norm[rows, :] * keep + jnp.sum(weights, axis=-1, keepdims=True)
        both = acc[rows, :] * keep + dot(weights.astype(BF16), kv[1, early:, :])
        qq[rows, :] = (both * (1.0 / total)).astype(BF16)
        return carry

    lax.fori_loop(0, qq.shape[0] // part, attend_early, 0)

    @pl.when(core == 1)
    def _():
        each(1, PARTS, lambda o: second_arrived(last, 0, o))
        each(0, PARTS, lambda o: second_arrived(last, 1, o))
        for line in range(2):
            each(1, PARTS, lambda o: share(last, line, (own_p + o) % PARTS).wait_recv())
        for line in range(2, 4):
            each(0, PARTS, lambda p: share(last, line, p).wait_recv())

    @pl.when(core == 0)
    def _():
        stage_three(last)
        for line in (0, 2):
            each(1, PARTS, lambda o: share(last, line, (own_p + o) % PARTS).wait_recv())
        for line in (1, 3):
            each(0, PARTS, lambda p: share(last, line, p).wait_recv())

    project(last, 0)
    project(last, 1)
    lax.fori_loop(0, qq.shape[0] // part, attend_late, 0)
    result = fold_heads(qq[...], heads)
    for l in range(lat_count):
        msend[l] = result[l * lat_rows : (l + 1) * lat_rows]
    mix_copies = []
    for i, peer in enumerate((partner, lat_y, diag)):
        mix_copies.append(remote(msend.at[peer], mrecv.at[lat], m_send.at[i], m_recv.at[i], (dp, peer)))
        mix_copies[-1].start()
    mrecv[lat] = msend[lat]
    loads[7].wait()
    loads[6].wait()
    wo_first[0].wait_recv()
    wo_relay.wait_recv()
    for copy in mix_copies:
        copy.wait_recv()
    total = dot(mrecv[0], w_og[0])
    for l in range(1, lat_count):
        total = total + dot(mrecv[l], w_og[l])
    final = (lmid[...].astype(F32) + total).astype(BF16)
    lat_out[...] = final
    lfin[...] = dot(rms_norm(final, g_wlat[...]), w_kvw[...]).astype(BF16)

    heads = width // HEAD
    for g in range(groups):
        rows = pl.ds(g * G, G)
        lrows = pl.ds(g * NLAT, NLAT)
        keys = spread_heads(lfin[lrows, :width], heads)
        values = spread_heads(lfin[lrows, width:], heads)
        scores = dot_nt(keys, tok_out[rows, :]).reshape(heads, NLAT, G)
        peak = jnp.max(scores, axis=1, keepdims=True)
        weights = jnp.exp(scores - peak)
        weights = weights * (1.0 / jnp.sum(weights, axis=1, keepdims=True))
        written = dot_tn(weights.reshape(heads * NLAT, G).astype(BF16), values)
        tok_out[rows, :] = (mid[rows, :].astype(F32) + written).astype(BF16)

    for copy in wo_first + [wo_relay] + mix_copies:
        copy.wait_send()
    for g in range(groups):
        each(1, nz, lambda offset: z_copy(g, offset).wait_send())

        def sent(p):
            on_first(g, p).wait_send()
            for half in range(2):
                on_second(g, half, p).wait_send()
            for line in range(4):
                share(g, line, p).wait_send()

        each(0, PARTS, sent)


def local(
    tokens, latents, gain_self, w_qkv_tok, w_o_tok, gain_read, w_kv_read, gain_lat, w_q_read,
    gain_glob, w_qkv_glob, w_o_glob, gain_write, w_q_write, gain_wlat, w_kv_write,
):
    dp_count = lax.axis_size("dp")
    lat_count = lax.axis_size("lat")
    rows, width = tokens.shape
    lat_rows, lat_width = latents.shape
    groups = rows // G
    here = w_qkv_glob.shape[2]
    nz = dp_count // 2
    all_rows = lat_rows * dp_count * lat_count
    vmem = pl.BlockSpec(memory_space=pltpu.VMEM)
    hbm = pl.BlockSpec(memory_space=pl.ANY)
    dma = pltpu.SemaphoreType.DMA
    return pl.pallas_call(
        functools.partial(kernel, dp_count, lat_count),
        out_shape=(
            jax.ShapeDtypeStruct(tokens.shape, BF16),
            jax.ShapeDtypeStruct(latents.shape, BF16),
        ),
        in_specs=[vmem, vmem, vmem, hbm, hbm, vmem, hbm, vmem, hbm, vmem, hbm, hbm, vmem, hbm, vmem, hbm],
        out_specs=(vmem, vmem),
        scratch_shapes=[
            pltpu.VMEM(w_qkv_tok.shape, BF16),
            pltpu.VMEM(w_o_tok.shape, BF16),
            pltpu.VMEM(w_kv_read.shape, BF16),
            pltpu.VMEM(w_q_read.shape, BF16),
            pltpu.VMEM(w_qkv_glob.shape, BF16),
            pltpu.VMEM((lat_count,) + w_o_glob.shape, BF16),
            pltpu.VMEM(w_q_write.shape, BF16),
            pltpu.VMEM(w_kv_write.shape, BF16),
            pltpu.VMEM(tokens.shape, BF16),
            pltpu.VMEM(latents.shape, BF16),
            pltpu.VMEM(latents.shape, BF16),
            pltpu.VMEM((G, w_qkv_tok.shape[1]), BF16),
            pltpu.VMEM((G, width), BF16),
            pltpu.VMEM((G, w_kv_read.shape[1]), BF16),
            pltpu.VMEM((groups, 2, 4 * nz, NLAT, lat_width), BF16),
            pltpu.VMEM((2, all_rows, here), BF16),
            pltpu.VMEM((lat_rows * lat_count * (here // HEAD), here), BF16),
            pltpu.VMEM((lat_count, lat_rows, here), BF16),
            pltpu.VMEM((lat_count, lat_rows, here), BF16),
            pltpu.VMEM((lat_rows, w_kv_write.shape[1]), BF16),
            pltpu.VMEM((lat_rows * lat_count * (here // HEAD), 1), F32),
            pltpu.VMEM((lat_rows * lat_count * (here // HEAD), 1), F32),
            pltpu.VMEM((lat_rows * lat_count * (here // HEAD), here), F32),
            dma((8,)),
            dma((groups, nz)),
            dma((groups, nz)),
            dma((groups, PARTS)),
            dma((groups, PARTS)),
            dma((groups, 2 * PARTS)),
            dma((groups, 2 * PARTS)),
            dma((groups, 4 * PARTS)),
            dma((groups, 4 * PARTS)),
            dma((3,)),
            dma((3,)),
            dma((3,)),
            dma((3,)),
        ],
        compiler_params=pltpu.CompilerParams(
            collective_id=0, has_side_effects=True, vmem_limit_bytes=67043328
        ),
    )(
        tokens, latents, gain_self[None], w_qkv_tok, w_o_tok, gain_read[None], w_kv_read,
        gain_lat[None], w_q_read, gain_glob[None], w_qkv_glob, w_o_glob, gain_write[None],
        w_q_write, gain_wlat[None], w_kv_write,
    )


def solution(mesh):
    rows = P(("dp", "lat"), None)
    whole = P()
    placed = (
        rows, rows, whole, whole, whole, whole, whole, whole, whole, whole,
        P(None, None, "lat"), P("lat", None), whole, whole, whole, whole,
    )
    return jax.shard_map(
        local, mesh=mesh, in_specs=placed, out_specs=(rows, rows), check_vma=False
    )
```

```python
import functools

import jax
import jax.numpy as jnp
from jax import lax
from jax.experimental import pallas as pl
from jax.experimental.pallas import tpu as pltpu
from jax.sharding import PartitionSpec as P

HEAD = 64
G = 256
NLAT = 16
SCALE = HEAD ** (-0.5)
MESH = pl.DeviceIdType.MESH
PARTS = 4
F32 = jnp.float32
BF16 = jnp.bfloat16


def rms_norm(values, gain):
    floats = values.astype(F32)
    factor = lax.rsqrt(jnp.mean(floats * floats, axis=-1, keepdims=True) + 1e-06)
    return (floats * factor * gain).astype(BF16)


def dot(a, b):
    return jnp.dot(a, b, preferred_element_type=F32)


def dot_nt(a, b):
    return lax.dot_general(a, b, (((1,), (1,)), ((), ())), preferred_element_type=F32)


def dot_tn(a, b):
    return lax.dot_general(a, b, (((0,), (0,)), ((), ())), preferred_element_type=F32)


def spread_heads(query, count):
    lane_head = lax.broadcasted_iota(jnp.int32, query.shape, 1) // HEAD
    zero = jnp.zeros_like(query)
    return jnp.concatenate([jnp.where(lane_head == h, query, zero) for h in range(count)], axis=0)


def fold_heads(stacked, count):
    rows = stacked.shape[0] // count
    lane_head = lax.broadcasted_iota(jnp.int32, (rows, stacked.shape[1]), 1) // HEAD
    out = stacked[:rows]
    for h in range(1, count):
        out = jnp.where(lane_head == h, stacked[h * rows : (h + 1) * rows], out)
    return out


def softmax_mix(stacked, keys, values):
    scores = dot_nt(stacked, keys)
    peak = jnp.max(scores, axis=-1, keepdims=True)
    weights = jnp.exp(scores - peak)
    total = jnp.sum(weights, axis=-1, keepdims=True)
    return dot(weights.astype(BF16), values) * (1.0 / total)


def kernel(
    dp_count,
    lat_count,
    tok,
    lat_in,
    g_self,
    w_qkv_h,
    w_o_h,
    g_read,
    w_kvr_h,
    g_lat,
    w_qr_h,
    g_glob,
    w_glob_h,
    w_og_h,
    g_write,
    w_qw_h,
    g_wlat,
    w_kvw_h,
    tok_out,
    lat_out,
    mid,
    lfin,
    w_qkv,
    w_o,
    w_kvr,
    w_qr,
    w_glob,
    w_og,
    w_qw,
    w_kvw,
    lmid,
    rq,
    packed,
    mixed,
    kvr,
    gath,
    kv,
    qq,
    msend,
    mrecv,
    top,
    norm,
    acc,
    load_sem,
    z_send,
    z_recv,
    f_send,
    f_recv,
    s_send,
    s_recv,
    c_send,
    c_recv,
    wo_send,
    wo_recv,
    m_send,
    m_recv,
):
    width = tok.shape[1]
    lat_width = lat_in.shape[1]
    groups = tok.shape[0] // G
    lat_rows = lat_in.shape[0]
    nz = dp_count // 2
    dp = lax.axis_index("dp")
    lat = lax.axis_index("lat")
    z, x = dp // 2, dp % 2
    y, core = lat // 2, lat % 2
    dp_x = dp + 1 - 2 * x
    lat_y = (lat + 2) % 4
    partner = lat + 1 - 2 * core
    diag = (partner + 2) % 4
    a = (1 - core) * y + core * x
    b = (1 - core) * x + core * y
    first = ((1 - core) * dp + core * dp_x, (1 - core) * lat_y + core * lat)
    second = ((1 - core) * dp_x + core * dp, (1 - core) * lat + core * lat_y)
    base = (b * 2 + a) * nz
    other = (b * 2 + 1 - a) * nz
    me = base + z
    far = (1 - 2 * b) * 2 * nz
    run = nz // PARTS

    loads = []
    for i, (src, dst) in enumerate(
        ((w_qkv_h, w_qkv), (w_o_h, w_o), (w_qr_h, w_qr), (w_kvr_h, w_kvr), (w_glob_h, w_glob),
         (w_qw_h, w_qw), (w_kvw_h, w_kvw), (w_og_h, w_og.at[lat]))
    ):
        loads.append(pltpu.make_async_copy(src, dst, load_sem.at[i]))
        loads[-1].start()

    barrier = pltpu.get_barrier_semaphore()

    def greet(offset, carry):
        pl.semaphore_signal(
            barrier, inc=1, device_id=((z + offset) % nz * 2 + x, lat), device_id_type=MESH
        )
        return carry

    lax.fori_loop(1, nz, greet, 0)
    for peer in ((dp_x, lat), (dp, lat_y), (dp, partner), (dp, diag)):
        pl.semaphore_signal(barrier, inc=1, device_id=peer, device_id_type=MESH)
    pl.semaphore_wait(barrier, nz + 3)

    def remote(src, dst, send_sem, recv_sem, peer):
        return pltpu.make_async_remote_copy(
            src_ref=src, dst_ref=dst, send_sem=send_sem, recv_sem=recv_sem, device_id=peer,
            device_id_type=MESH,
        )

    wo_first = [
        remote(w_og_h, w_og.at[lat], wo_send.at[0], wo_recv.at[0], (dp, partner)),
        remote(w_og_h, w_og.at[lat], wo_send.at[1], wo_recv.at[1], (dp, lat_y)),
    ]
    wo_relay = remote(w_og.at[lat_y], w_og.at[lat_y], wo_send.at[2], wo_recv.at[2], (dp, partner))
    for copy in wo_first:
        copy.start()

    def piece(g, start, count):
        return gath.at[g, core, pl.ds(start, count)]

    def along(ref, send_sem, recv_sem, peer):
        return remote(ref, ref, send_sem, recv_sem, peer)

    def on_first(g, p):
        return along(
            piece(g, base + p * run, run), f_send.at[g, p], f_recv.at[g, p], first
        )

    def on_second(g, half, p):
        start = base + (other - base) * half + p * run
        k = half * PARTS + p
        return along(piece(g, start, run), s_send.at[g, k], s_recv.at[g, k], second)

    def share(g, line, p):
        start = (base, other, base + far, other + far)[line] + p * run
        k = line * PARTS + p
        return along(
            piece(g, start, run), c_send.at[g, k], c_recv.at[g, k], (dp, partner)
        )

    def z_copy(g, offset):
        return remote(
            gath.at[g, core, me], gath.at[g, core, me], z_send.at[g, (z + offset) % nz],
            z_recv.at[g, z], ((z + offset) % nz * 2 + x, lat),
        )

    def each(low, high, body):
        def one(i, carry):
            body(i)
            return carry

        lax.fori_loop(low, high, one, 0)

    def z_start(g):
        each(1, nz, lambda offset: z_copy(g, offset).start())

    def z_arrived(g, block):
        ref = piece(g, base + block, 1)

        @pl.when(block != z)
        def _():
            pltpu.make_async_copy(ref, ref, z_recv.at[g, block]).wait()

    def stage_one(g, low, high):
        def body(o):
            p = (z // run + o) % PARTS
            each(0, run, lambda i: z_arrived(g, p * run + i))
            on_first(g, p).start()
            on_second(g, 0, p).start()
            share(g, 0, p).start()

        each(low, high, body)

    def stage_two(g):
        def body(o):
            p = (z // run + o) % PARTS
            on_first(g, p).wait_recv()
            on_second(g, 1, p).start()
            share(g, 1, p).start()

        each(0, PARTS, body)

    def second_arrived(g, half, o):
        p = (z // run + o) % PARTS
        on_second(g, half, p).wait_recv()
        share(g, 2 + half, p).start()

    def stage_three(g):
        for half in range(2):
            each(0, PARTS, lambda o: second_arrived(g, half, o))

    def gathered(g):
        for line in range(4):
            each(0, PARTS, lambda p: share(g, line, p).wait_recv())

    def self_part(g):
        rows = pl.ds(g * G, G)
        group = tok[rows, :]
        normed = rms_norm(group, g_self[...])
        if g == 0:
            loads[0].wait()
        packed[...] = dot(normed, w_qkv[...]).astype(BF16)
        for pair in range(width // (2 * HEAD)):
            at = pair * 2 * HEAD
            query = packed[:, at : at + 2 * HEAD] * jnp.asarray(SCALE, BF16)
            keys = packed[:, width + at : width + at + 2 * HEAD]
            values = packed[:, 2 * width + at : 2 * width + at + 2 * HEAD]
            out = softmax_mix(spread_heads(query, 2), keys, values)
            mixed[:, at : at + 2 * HEAD] = fold_heads(out, 2).astype(BF16)
        if g == 0:
            loads[1].wait()
        mid[rows, :] = (group.astype(F32) + dot(mixed[...], w_o[...])).astype(BF16)

    def read_part(g):
        if g == 0:
            loads[2].wait()
            query = dot(rms_norm(lat_in[...], g_lat[...]), w_qr[...]).astype(BF16)
            rq[...] = query * jnp.asarray(SCALE, BF16)
            loads[3].wait()
        rows = pl.ds(g * G, G)
        lrows = pl.ds(g * NLAT, NLAT)
        kvr[...] = dot(rms_norm(mid[rows, :], g_read[...]), w_kvr[...]).astype(BF16)
        quad = 4 * HEAD
        for at in range(0, lat_width, quad):
            out = softmax_mix(
                spread_heads(rq[lrows, at : at + quad], 4),
                kvr[:, at : at + quad],
                kvr[:, lat_width + at : lat_width + at + quad],
            )
            lmid[lrows, at : at + quad] = (
                lat_in[lrows, at : at + quad].astype(F32) + fold_heads(out, 4)
            ).astype(BF16)
        gath[g, core, me] = rms_norm(lmid[lrows, :], g_glob[...])
        z_start(g)
        stage_one(g, 0, 1)

    last = groups - 1
    for g in range(groups):
        self_part(g)
        if g >= 2:
            stage_one(g - 2, 1, PARTS)
            if g == 2:
                wo_first[1].wait_recv()
                wo_relay.start()
        read_part(g)

    block_rows = 4 * nz * NLAT
    tile = min(block_rows, G)
    blocks = tile // NLAT

    def project(g, c):
        def one(i, carry):
            rows = gath[g, c, pl.ds(i * blocks, blocks)].reshape(tile, lat_width)
            at = pl.multiple_of((g * 2 + c) * block_rows + i * tile, tile)
            kv[0, pl.ds(at, tile), :] = dot(rows, w_glob[1]).astype(BF16)
            kv[1, pl.ds(at, tile), :] = dot(rows, w_glob[2]).astype(BF16)
            return carry

        lax.fori_loop(0, block_rows // tile, one, 0)

    for g in range(last - 1):
        stage_two(g)
    loads[5].wait()
    for g in range(groups):
        rows = pl.ds(g * G, G)
        query = dot(rms_norm(mid[rows, :], g_write[...]), w_qw[...]).astype(BF16)
        tok_out[rows, :] = query * jnp.asarray(SCALE, BF16)
    stage_one(last - 1, 1, PARTS)
    loads[4].wait()
    for g in range(last - 1):
        stage_three(g)
    stage_two(last - 1)
    for g in range(last - 1):
        gathered(g)
        project(g, 0)
        project(g, 1)
    stage_one(last, 1, PARTS)
    stage_two(last)
    stage_three(last - 1)
    gathered(last - 1)
    project(last - 1, 0)
    project(last - 1, 1)
    own_p = z // run

    @pl.when(core == 1)
    def _():
        on_second(last, 0, own_p).wait_recv()
        share(last, 2, own_p).start()
        for line in range(2):
            share(last, line, own_p).wait_recv()

    @pl.when(core == 0)
    def _():
        for line in (0, 2):
            share(last, line, own_p).wait_recv()

    own = []
    for l in range(lat_count):
        ly, lc = l // 2, l % 2
        index = ((x * 2 + ly) if lc == 0 else (ly * 2 + x)) * nz + z
        for g in range(groups):
            own.append(gath[g, lc, index])
    query = dot(jnp.concatenate(own, axis=0), w_glob[0]).astype(BF16) * jnp.asarray(SCALE, BF16)
    heads = query.shape[1] // HEAD
    qq[...] = spread_heads(query, heads)
    early = last * 2 * block_rows
    full = lat_rows * lat_count
    part = full if early * full <= 2**20 else lat_rows

    def attend_early(i, carry):
        rows = pl.ds(pl.multiple_of(i * part, part), part)
        scores = dot_nt(qq[rows, :], kv[0, :early, :])
        peak = jnp.max(scores, axis=-1, keepdims=True)
        weights = jnp.exp(scores - peak)
        top[rows, :] = peak
        norm[rows, :] = jnp.sum(weights, axis=-1, keepdims=True)
        acc[rows, :] = dot(weights.astype(BF16), kv[1, :early, :])
        return carry

    def attend_late(i, carry):
        rows = pl.ds(pl.multiple_of(i * part, part), part)
        scores = dot_nt(qq[rows, :], kv[0, early:, :])
        peak = jnp.maximum(top[rows, :], jnp.max(scores, axis=-1, keepdims=True))
        weights = jnp.exp(scores - peak)
        keep = jnp.exp(top[rows, :] - peak)
        total = norm[rows, :] * keep + jnp.sum(weights, axis=-1, keepdims=True)
        both = acc[rows, :] * keep + dot(weights.astype(BF16), kv[1, early:, :])
        qq[rows, :] = (both * (1.0 / total)).astype(BF16)
        return carry

    lax.fori_loop(0, qq.shape[0] // part, attend_early, 0)

    @pl.when(core == 1)
    def _():
        each(1, PARTS, lambda o: second_arrived(last, 0, o))
        each(0, PARTS, lambda o: second_arrived(last, 1, o))
        for line in range(2):
            each(1, PARTS, lambda o: share(last, line, (own_p + o) % PARTS).wait_recv())
        for line in range(2, 4):
            each(0, PARTS, lambda p: share(last, line, p).wait_recv())

    @pl.when(core == 0)
    def _():
        stage_three(last)
        for line in (0, 2):
            each(1, PARTS, lambda o: share(last, line, (own_p + o) % PARTS).wait_recv())
        for line in (1, 3):
            each(0, PARTS, lambda p: share(last, line, p).wait_recv())

    project(last, 0)
    project(last, 1)
    lax.fori_loop(0, qq.shape[0] // part, attend_late, 0)
    result = fold_heads(qq[...], heads)
    for l in range(lat_count):
        msend[l] = result[l * lat_rows : (l + 1) * lat_rows]
    mix_copies = []
    for i, peer in enumerate((partner, lat_y, diag)):
        mix_copies.append(remote(msend.at[peer], mrecv.at[lat], m_send.at[i], m_recv.at[i], (dp, peer)))
        mix_copies[-1].start()
    mrecv[lat] = msend[lat]
    loads[7].wait()
    loads[6].wait()
    wo_first[0].wait_recv()
    wo_relay.wait_recv()
    for copy in mix_copies:
        copy.wait_recv()
    total = dot(mrecv[0], w_og[0])
    for l in range(1, lat_count):
        total = total + dot(mrecv[l], w_og[l])
    final = (lmid[...].astype(F32) + total).astype(BF16)
    lat_out[...] = final
    lfin[...] = dot(rms_norm(final, g_wlat[...]), w_kvw[...]).astype(BF16)

    for copy in wo_first + [wo_relay] + mix_copies:
        copy.wait_send()
    for g in range(groups):
        each(1, nz, lambda offset: z_copy(g, offset).wait_send())

        def sent(p):
            on_first(g, p).wait_send()
            for half in range(2):
                on_second(g, half, p).wait_send()
            for line in range(4):
                share(g, line, p).wait_send()

        each(0, PARTS, sent)


def back(query, final, mid, key_vals, tok_out, lat_out):
    width = query.shape[1]
    heads = width // HEAD
    keys = spread_heads(key_vals[:, :width], heads)
    values = spread_heads(key_vals[:, width:], heads)
    scores = dot_nt(keys, query[...]).reshape(heads, NLAT, G)
    peak = jnp.max(scores, axis=1, keepdims=True)
    weights = jnp.exp(scores - peak)
    weights = weights * (1.0 / jnp.sum(weights, axis=1, keepdims=True))
    written = dot_tn(weights.reshape(heads * NLAT, G).astype(BF16), values)
    tok_out[...] = (mid[...].astype(F32) + written).astype(BF16)
    lat_out[...] = final[...]


def local(
    tokens, latents, gain_self, w_qkv_tok, w_o_tok, gain_read, w_kv_read, gain_lat, w_q_read,
    gain_glob, w_qkv_glob, w_o_glob, gain_write, w_q_write, gain_wlat, w_kv_write,
):
    dp_count = lax.axis_size("dp")
    lat_count = lax.axis_size("lat")
    rows, width = tokens.shape
    lat_rows, lat_width = latents.shape
    groups = rows // G
    here = w_qkv_glob.shape[2]
    nz = dp_count // 2
    all_rows = lat_rows * dp_count * lat_count
    vmem = pl.BlockSpec(memory_space=pltpu.VMEM)
    hbm = pl.BlockSpec(memory_space=pl.ANY)
    dma = pltpu.SemaphoreType.DMA
    query, final, mid, key_vals = pl.pallas_call(
        functools.partial(kernel, dp_count, lat_count),
        out_shape=(
            jax.ShapeDtypeStruct(tokens.shape, BF16),
            jax.ShapeDtypeStruct(latents.shape, BF16),
            jax.ShapeDtypeStruct(tokens.shape, BF16),
            jax.ShapeDtypeStruct((lat_rows, w_kv_write.shape[1]), BF16),
        ),
        in_specs=[vmem, vmem, vmem, hbm, hbm, vmem, hbm, vmem, hbm, vmem, hbm, hbm, vmem, hbm, vmem, hbm],
        out_specs=(vmem,) * 4,
        scratch_shapes=[
            pltpu.VMEM(w_qkv_tok.shape, BF16),
            pltpu.VMEM(w_o_tok.shape, BF16),
            pltpu.VMEM(w_kv_read.shape, BF16),
            pltpu.VMEM(w_q_read.shape, BF16),
            pltpu.VMEM(w_qkv_glob.shape, BF16),
            pltpu.VMEM((lat_count,) + w_o_glob.shape, BF16),
            pltpu.VMEM(w_q_write.shape, BF16),
            pltpu.VMEM(w_kv_write.shape, BF16),
            pltpu.VMEM(latents.shape, BF16),
            pltpu.VMEM(latents.shape, BF16),
            pltpu.VMEM((G, w_qkv_tok.shape[1]), BF16),
            pltpu.VMEM((G, width), BF16),
            pltpu.VMEM((G, w_kv_read.shape[1]), BF16),
            pltpu.VMEM((groups, 2, 4 * nz, NLAT, lat_width), BF16),
            pltpu.VMEM((2, all_rows, here), BF16),
            pltpu.VMEM((lat_rows * lat_count * (here // HEAD), here), BF16),
            pltpu.VMEM((lat_count, lat_rows, here), BF16),
            pltpu.VMEM((lat_count, lat_rows, here), BF16),
            pltpu.VMEM((lat_rows * lat_count * (here // HEAD), 1), F32),
            pltpu.VMEM((lat_rows * lat_count * (here // HEAD), 1), F32),
            pltpu.VMEM((lat_rows * lat_count * (here // HEAD), here), F32),
            dma((8,)),
            dma((groups, nz)),
            dma((groups, nz)),
            dma((groups, PARTS)),
            dma((groups, PARTS)),
            dma((groups, 2 * PARTS)),
            dma((groups, 2 * PARTS)),
            dma((groups, 4 * PARTS)),
            dma((groups, 4 * PARTS)),
            dma((3,)),
            dma((3,)),
            dma((3,)),
            dma((3,)),
        ],
        compiler_params=pltpu.CompilerParams(
            collective_id=0, has_side_effects=True, vmem_limit_bytes=67043328
        ),
    )(
        tokens, latents, gain_self[None], w_qkv_tok, w_o_tok, gain_read[None], w_kv_read,
        gain_lat[None], w_q_read, gain_glob[None], w_qkv_glob, w_o_glob, gain_write[None],
        w_q_write, gain_wlat[None], w_kv_write,
    )
    per_group = pl.BlockSpec((G, width), lambda g: (g, 0))
    per_lat = pl.BlockSpec((NLAT, lat_width), lambda g: (g, 0))
    return pl.pallas_call(
        back,
        grid=(groups,),
        out_shape=(
            jax.ShapeDtypeStruct(tokens.shape, BF16),
            jax.ShapeDtypeStruct(latents.shape, BF16),
        ),
        in_specs=[
            per_group,
            per_lat,
            per_group,
            pl.BlockSpec((NLAT, key_vals.shape[1]), lambda g: (g, 0)),
        ],
        out_specs=(per_group, per_lat),
    )(query, final, mid, key_vals)


def solution(mesh):
    rows = P(("dp", "lat"), None)
    whole = P()
    placed = (
        rows, rows, whole, whole, whole, whole, whole, whole, whole, whole,
        P(None, None, "lat"), P("lat", None), whole, whole, whole, whole,
    )
    return jax.shard_map(
        local, mesh=mesh, in_specs=placed, out_specs=(rows, rows), check_vma=False
    )
```
